32 devices in a mesh: keys: 8 (over z, y), tiles: 4 (over x, core).
Axes of the slice: x: 2, y: 2, z: 4, core: 2. Of those that a mesh axis runs over, the one named last changes fastest.
Arguments:
- fact_store: int32 [131072], P(('keys', 'tiles')), may hold values from 0 to 2047, as said below
- fact_item: int32 [131072], P(('keys', 'tiles')), may hold values from 0 to 4095, as said below
- store_count: int32 [2048], P('keys'), may hold values from 1 to 64, as said below
- store_table: bfloat16 [2048, 1024], P('keys'), may hold values from -6 to 6
- item_table: bfloat16 [4096, 1024], P('tiles'), may hold values from -6 to 6
Outputs:
- gram_left: float32 [1024, 2048], P('keys', 'tiles')
- gram_items: float32 [1024, 1024], P('keys', 'tiles')
The draws below stay inside these ranges and needn't reach their ends.
Inputs may be any that keep to these rules, and one draw needn't show every extreme that they name: `fact_store`: every fact row held by keys index g names a store of g * 256 to (g + 1) * 256 - 1. `fact_item`: every fact row held by tiles index t names an item of t * 1024 to (t + 1) * 1024 - 1. `store_count`: each a power of two.
All inputs are finite; a program needn't handle non-finite values.
Results may differ from the reference program's by a relative error of at most 0.0003.
Values sent between devices are 32-bit elements; how exact they have to be, the bound alone decides.
No kernel may reach another device: no remote copies, remote signals or barrier semaphores. Data moves between devices by JAX's collectives and lax.ppermute only.
A program may use at most 64 MiB of HBM per device.

```python
import jax
import jax.numpy as jnp
from jax import lax

DA = 1024
DB = 1024
KEY_DEV = 256
ITEM_DEV = 1024
ROW_DEV = 4096
KEYS = 2048
ITEMS = 4096
FACT = 131072


def joint_rows(key):
    base = jax.random.fold_in(key, 7)
    first, second, third, fourth = jax.random.split(base, 4)
    tiles_count = ITEMS // ITEM_DEV
    row = jnp.arange(FACT, dtype=jnp.int32)
    device = row // ROW_DEV
    group = device // tiles_count
    tile = device % tiles_count
    local = jnp.minimum(jax.random.randint(first, (FACT,), 0, KEY_DEV), jax.random.randint(second, (FACT,), 0, KEY_DEV))
    store = group * KEY_DEV + local
    anchor = jax.random.randint(third, (KEYS,), 0, ITEM_DEV)
    offset = jax.random.randint(fourth, (FACT,), 0, 8)
    item = tile * ITEM_DEV + (jnp.take(anchor, store, axis=0) + offset) % ITEM_DEV
    return (store.astype(jnp.int32), item.astype(jnp.int32))


def draw_fact_store(key, part):
    return joint_rows(key)[0]


def draw_fact_item(key, part):
    return joint_rows(key)[1]


def draw_store_count(key, part):
    power = jax.random.randint(jax.random.fold_in(key, 11), (KEYS,), 0, 7)
    counts = jnp.left_shift(jnp.ones((KEYS,), jnp.int32), power)
    return counts.at[0].set(64).at[1].set(1)


def level_of(rng, dims, cuts, low, top_value):
    loudness, own = 1.0, jax.random.fold_in(rng, 6)
    for axis_at, shards_of in cuts:
        draws = jnp.exp(jax.random.uniform(jax.random.fold_in(own, axis_at), (shards_of,), jnp.float32, low / len(cuts), top_value / len(cuts)))
        loudness = loudness * jnp.repeat(draws, dims[axis_at] // shards_of).reshape([-1 if axis == axis_at else 1 for axis in range(len(dims))])
    return loudness


def noise(key, dims, scale, limit, cuts=(), held_as=jnp.bfloat16):
    result = jax.random.normal(key, dims, jnp.float32) * scale
    if len(cuts) > 0:
        result = level_of(key, dims, cuts, -0.22, 0.18) * result
    return jnp.clip(result, min=-limit, max=limit).astype(held_as)


def setup_inputs(seed: int = 0) -> dict:
    seeds = jax.random.split(jax.random.key(seed), 6)
    fact_store = draw_fact_store(jax.random.fold_in(seeds[5], 71), 0)
    fact_item = draw_fact_item(jax.random.fold_in(seeds[5], 71), 0)
    store_count = draw_store_count(jax.random.fold_in(seeds[5], 71), 0)
    store_table = noise(seeds[3], (KEYS, DA), 1.0, 6.0, ((0, 8),))
    item_table = noise(seeds[4], (ITEMS, DB), 1.0, 6.0, ((0, 4),))
    return dict(fact_store=fact_store, fact_item=fact_item, store_count=store_count, store_table=store_table, item_table=item_table)


def reference(fact_store, fact_item, store_count, store_table, item_table):
    row_weight = jnp.take(store_count, fact_store, axis=0).astype(jnp.float32)
    store_weight = jax.ops.segment_sum(row_weight, fact_store, num_segments=KEYS)
    item_weight = jax.ops.segment_sum(row_weight, fact_item, num_segments=ITEMS)
    total = jnp.sum(store_weight)
    flat_index = fact_store * ITEMS + fact_item
    pairs = jax.ops.segment_sum(row_weight, flat_index, num_segments=KEYS * ITEMS).reshape(KEYS, ITEMS)
    item_float = item_table.astype(jnp.float32)
    store_float = store_table.astype(jnp.float32)
    aggregate = jnp.dot(pairs, item_float, precision=lax.Precision.HIGHEST)
    combined = jnp.concatenate([store_weight[:, None] * store_float, aggregate], axis=1)
    gram_left = jnp.dot(store_float.T, combined, precision=lax.Precision.HIGHEST) / total
    gram_items = jnp.dot(item_float.T, item_weight[:, None] * item_float, precision=lax.Precision.HIGHEST) / total
    return gram_left, gram_items
```

```python
import functools
import math

import jax
import jax.numpy as jnp
from jax import lax
from jax.experimental import pallas as pl
from jax.experimental.pallas import tpu as pltpu
from jax.sharding import PartitionSpec as P

NT = (((1,), (1,)), ((), ()))
F32, BF16 = jnp.float32, jnp.bfloat16
LANES = 128


def call(kernel, outs, *args, scratch=(), flops=0, pinned=True):
    whole = pl.BlockSpec(memory_space=pltpu.VMEM)
    shapes = [(pltpu.VMEM if pinned else jax.ShapeDtypeStruct)(shape, kind) for shape, kind in outs]
    moved = sum(a.size * a.dtype.itemsize for a in args)
    moved += sum(math.prod(shape) * jnp.dtype(kind).itemsize for shape, kind in outs)
    return pl.pallas_call(
        kernel,
        out_shape=shapes,
        in_specs=[whole] * len(args),
        out_specs=[whole] * len(outs),
        scratch_shapes=list(scratch),
        compiler_params=pltpu.CompilerParams(vmem_limit_bytes=24 << 20),
        cost_estimate=pl.CostEstimate(flops=flops, bytes_accessed=moved, transcendentals=0),
    )(*args)


def dot(a, b):
    return jnp.dot(a, b, preferred_element_type=F32)


def split(value):
    high = value.astype(BF16)
    return high, (value - high.astype(F32)).astype(BF16)


def one_hot(ids, size):
    row = lax.broadcasted_iota(jnp.int32, (size, ids.shape[1]), 0)
    return jnp.where(row == lax.rem(ids, size), 1.0, 0.0).astype(BF16)


def count_kernel(store_ref, out_ref):
    hits = one_hot(store_ref[...], out_ref.shape[1])
    ones = jnp.ones((out_ref.shape[0], hits.shape[1]), BF16)
    out_ref[...] = lax.dot_general(ones, hits, NT, preferred_element_type=F32)


def left_kernel(rows, table_ref, scale_ref, out_ref, turned_ref):
    key = lax.axis_index("keys")
    turned_ref[...] = (table_ref[...].astype(F32).T * scale_ref[...].astype(F32)).astype(BF16)
    for r in range(out_ref.shape[0] // rows):
        at = pl.ds(pl.multiple_of((key ^ r) * rows, rows), rows)
        out_ref[r * rows : (r + 1) * rows] = turned_ref[at]


def place(t, tiles):
    return 2 * (t % (tiles // 2)) + t // (tiles // 2)


def levels(order):
    if not order:
        return [[0]]
    rest = levels(order[1:])
    return [[order[0] ^ r for level in rest for r in level]] + rest


def store_levels(refs, order, rows, value_of):
    for ref, level in zip(refs, levels(order)):
        for i, r in enumerate(level):
            ref[i * rows : (i + 1) * rows] = value_of(r)


def level_shapes(order, rows, columns):
    return [((len(level) * rows, columns), F32) for level in levels(order)]


def pair_kernel(step, orders, store_ref, item_ref, scale_ref, table_ref, weight_ref, *refs):
    acc_ref, high_ref, low_ref = refs[-3:]
    rows, width = acc_ref.shape[0], refs[0].shape[1]
    acc_ref[...] = jnp.zeros_like(acc_ref)

    @pl.loop(0, store_ref.shape[1] // step)
    def _(i):
        part = pl.ds(pl.multiple_of(i * step, step), step)
        stores = one_hot(store_ref[:, part], rows)
        items = one_hot(item_ref[:, part], acc_ref.shape[1])
        acc_ref[...] += lax.dot_general(stores, items, NT, preferred_element_type=F32)

    high_ref[...], low_ref[...] = split(acc_ref[...])
    scale = jnp.broadcast_to(scale_ref[...].astype(F32), (8, rows)).astype(BF16)
    weight = dot(scale, high_ref[...]) + dot(scale, low_ref[...])
    for i in range(weight_ref.shape[0]):
        weight_ref[i : i + 1] = weight[:1, i * LANES : (i + 1) * LANES]
    tile, tiles = lax.axis_index("tiles"), lax.axis_size("tiles")
    count = len(orders[0]) + 1
    for h, order in enumerate(orders):

        def aggregate(r, h=h):
            start = place(tile ^ r, tiles) * (len(orders) * width) + h * width
            right = table_ref[:, pl.ds(pl.multiple_of(start, LANES), width)]
            return dot(high_ref[...], right) + dot(low_ref[...], right)

        store_levels(refs[h * count : (h + 1) * count], order, rows, aggregate)


def square_kernel(orders, left_ref, one_ref, two_ref, scale_ref, table_ref, weight_ref, small_ref, *refs):
    counts = one_ref[...] + two_ref[...]
    total = jnp.sum(counts[:1] * scale_ref[...].astype(F32))
    items = weight_ref.shape[0]
    small_ref[:items] = weight_ref[...]
    small_ref[items:] = jnp.full((8, LANES), total, F32)
    tile, tiles = lax.axis_index("tiles"), lax.axis_size("tiles")
    width = refs[0].shape[1]
    count = len(orders[0]) + 1
    rows = refs[count - 1].shape[0]
    for h, order in enumerate(orders):
        start = place(tile, tiles) * (len(orders) * width) + h * width
        right = table_ref[:, pl.ds(pl.multiple_of(start, LANES), width)]

        def product(r, right=right):
            high, low = split(left_ref[r * rows : (r + 1) * rows].astype(F32) * counts[:1])
            return dot(high, right) + dot(low, right)

        store_levels(refs[h * count : (h + 1) * count], order, rows, product)


def cross_kernel(order, left_ref, one_ref, two_ref, *refs):
    high, low = split(one_ref[...] + two_ref[...])
    rows = refs[-1].shape[0]

    def product(r):
        left = left_ref[r * rows : (r + 1) * rows]
        return dot(left, high) + dot(left, low)

    store_levels(refs, order, rows, product)


def item_kernel(order, left_ref, small_ref, table_ref, *refs):
    weight = jnp.concatenate([small_ref[i : i + 1] for i in range(small_ref.shape[0] - 8)], axis=1)
    high, low = split(left_ref[...].astype(F32) * weight)
    tile = lax.axis_index("tiles")
    rows, width = refs[-1].shape

    def product(r):
        right = table_ref[:, pl.ds(pl.multiple_of((tile ^ r) * width, LANES), width)]
        return dot(high, right) + dot(low, right)

    store_levels(refs, order, rows, product)


def step_kernel(got_ref, *refs):
    half = len(refs) // 2
    at = 0
    for source, target in zip(refs[:half], refs[half:]):
        n = source.shape[0]
        target[...] = source[...] + got_ref[at : at + n]
        at += n


def swap(value, axis, bit):
    n = lax.axis_size(axis)
    return lax.ppermute(value, axis, [(i, i ^ bit) for i in range(n)])


def add(one, two):
    return call(step_kernel, [(one.shape, F32)], two, one)[0]


def scatter(parts, axis, order):
    for bit in order[:-1]:
        got = swap(parts[0], axis, bit)
        parts = call(step_kernel, [(p.shape, F32) for p in parts[1:]], got, *parts[1:])
    return parts[1], swap(parts[0], axis, order[-1])


def last_kernel(count, *refs):
    sends, mine = refs[-2:]
    width = sends.shape[1] // count
    upper = lax.axis_index("tiles") >= lax.axis_size("tiles") // 2
    for h in range(count):
        at = slice(h * width, (h + 1) * width)
        square = refs[2 * h][...] + refs[2 * h + 1][...]
        cross = refs[2 * (count + h)][...] + refs[2 * (count + h) + 1][...]
        sends[:, at] = jnp.where(upper, square, cross)
        mine[:, at] = jnp.where(upper, cross, square)


def place_kernel(mine_ref, got_ref, small_ref, out_ref):
    width = mine_ref.shape[1]
    upper = lax.axis_index("tiles") // (lax.axis_size("tiles") // 2)
    total = small_ref[small_ref.shape[0] - 1 :, :1]
    out_ref[:, pl.ds(pl.multiple_of(upper * width, LANES), width)] = mine_ref[...] / total
    out_ref[:, pl.ds(pl.multiple_of((1 - upper) * width, LANES), width)] = got_ref[...] / total


def divide_kernel(one_ref, two_ref, small_ref, out_ref):
    out_ref[...] = (one_ref[...] + two_ref[...]) / small_ref[small_ref.shape[0] - 1 :, :1]


def shards(fact_store, fact_item, store_count, store_table, item_table):
    key_dev, width_a = store_table.shape
    item_dev, width_b = item_table.shape
    facts = fact_store.shape[0]
    keys_count, tiles_count = lax.axis_size("keys"), lax.axis_size("tiles")
    block_a, block_b = width_a // keys_count, width_b // keys_count
    width = width_a // tiles_count
    streams = 2
    sub = width // streams
    store_row, item_row = fact_store.reshape(1, facts), fact_item.reshape(1, facts)
    scale_row = store_count.reshape(1, key_dev)
    key_bits = [1 << i for i in range(keys_count.bit_length() - 1)]
    tile_bits = [1 << i for i in range(tiles_count.bit_length() - 1)]
    orders = [key_bits, key_bits[1::-1] + key_bits[2:]]

    (counts,) = call(count_kernel, [((8, key_dev), F32)], store_row, flops=2 * 8 * facts * key_dev)
    for bit in tile_bits[:-1]:
        counts = add(counts, swap(counts, "tiles", bit))
    counts_got = swap(counts, "tiles", tile_bits[-1])

    (left,) = call(
        functools.partial(left_kernel, block_a),
        [((width_a, key_dev), BF16)],
        store_table,
        scale_row,
        scratch=[pltpu.VMEM((width_a, key_dev), BF16)],
    )
    item_left = lax.dynamic_slice_in_dim(item_table, lax.axis_index("keys") * block_b, block_b, 1).T

    weight, *parts = call(
        functools.partial(pair_kernel, min(facts, 2048), [tile_bits] * streams),
        [((item_dev // LANES, LANES), F32)] + level_shapes(tile_bits, key_dev, sub) * streams,
        store_row,
        item_row,
        scale_row,
        item_table,
        scratch=[
            pltpu.VMEM((key_dev, item_dev), F32),
            pltpu.VMEM((key_dev, item_dev), BF16),
            pltpu.VMEM((key_dev, item_dev), BF16),
        ],
        flops=2 * key_dev * item_dev * (facts + 2 * width_b),
    )
    n = len(tile_bits) + 1
    aggregates = [scatter(parts[h * n : (h + 1) * n], "tiles", tile_bits) for h in range(streams)]

    small, *parts = call(
        functools.partial(square_kernel, orders),
        [((item_dev // LANES + 8, LANES), F32)]
        + [s for order in orders for s in level_shapes(order, block_a, sub)],
        left,
        counts,
        counts_got,
        scale_row,
        store_table,
        weight,
        flops=4 * width_a * key_dev * width,
    )
    n = len(key_bits) + 1
    final = []
    for h, order in enumerate(orders):
        final += scatter(parts[h * n : (h + 1) * n], "keys", order)
    for bit in key_bits:
        small = add(small, swap(small, "keys", bit))

    for h, order in enumerate(orders):
        parts = call(
            functools.partial(cross_kernel, order),
            level_shapes(order, block_a, sub),
            left,
            *aggregates[h],
            flops=4 * width_a * key_dev * sub,
        )
        final += scatter(parts, "keys", order)

    parts = call(
        functools.partial(item_kernel, tile_bits),
        level_shapes(tile_bits, block_b, width_b // tiles_count),
        item_left,
        small,
        item_table,
        flops=4 * block_b * item_dev * width_b,
    )
    items = scatter(parts, "tiles", tile_bits)
    (items,) = call(divide_kernel, [(items[0].shape, F32)], *items, small, pinned=False)

    sends, mine = call(functools.partial(last_kernel, streams), [((block_a, width), F32)] * 2, *final)
    got = swap(sends, "tiles", tile_bits[-1])
    (left_out,) = call(place_kernel, [((block_a, 2 * width), F32)], mine, got, small, pinned=False)
    return left_out, items


def solution(mesh):
    placed = (
        P(("keys", "tiles")),
        P(("keys", "tiles")),
        P("keys"),
        P("keys", None),
        P("tiles", None),
    )
    return jax.shard_map(
        shards,
        mesh=mesh,
        in_specs=placed,
        out_specs=(P("keys", "tiles"), P("keys", "tiles")),
        check_vma=False,
    )
```
